128 devices in a mesh: pair: 16 (over x, z_lo, core), aux: 8 (over y, z_hi).
Axes of the slice: x: 4, y: 4, z: 4 (z_hi: 2, z_lo: 2; z = z_hi * 2 + z_lo), core: 2. Of those that a mesh axis runs over, the one named last changes fastest.
Arguments:
- integrals: bfloat16 [16, 2, 512, 256, 256], P('pair', None, 'aux'), may hold values from -6 to 6
- coef_table: bfloat16 [2048, 2, 128], P('pair'), may hold values from -0.375 to 0.375
- row_slot: int32 [2048], replicated, may hold values from 0 to 2047, each once
- pair_k: int32 [16, 2], P('pair'), may hold values from 0 to 7, as said below
Outputs:
- exchange_k: float32 [2, 8, 256, 256], P(None, None, 'aux', 'pair')
The draws below stay inside these ranges and needn't reach their ends.
Inputs may be any that keep to these rules, and one draw needn't show every extreme that they name: `row_slot`: each table row holds exactly one orbital row of one k-point. `pair_k`: the two k-points of a pair differ, and every k-point belongs to some listed pair.
All inputs are finite; a program needn't handle non-finite values.
Results may differ from the reference program's by a relative error of at most 0.0003.
Values may be sent and summed in bfloat16 or wider, within the bound.
A program may use at most 192 MiB of HBM per device.

```python
import jax
import jax.numpy as jnp
from jax import lax

NORB = 256
NOCC = 128
NKPT = 8
NPAIR = 16
NAUX = 512


def draw_pair_k(key, part):
    key_perm, key_first, key_offset = jax.random.split(jax.random.fold_in(key, 17), 3)
    shuffled = jax.random.permutation(key_perm, jnp.arange(NKPT, dtype=jnp.int32))
    covering = shuffled.reshape(NKPT // 2, 2)
    first_k = jax.random.randint(key_first, (NPAIR,), 0, NKPT, dtype=jnp.int32)
    offset = jax.random.randint(key_offset, (NPAIR,), 1, NKPT, dtype=jnp.int32)
    second_k = (first_k + offset) % NKPT
    random_pairs = jnp.stack([first_k, second_k], 1)
    position = jnp.arange(NPAIR, dtype=jnp.int32)
    chosen = covering[jnp.minimum(position, NKPT // 2 - 1)]
    return jnp.where(position[:, None] < NKPT // 2, chosen, random_pairs).astype(jnp.int32)


def with_spikes(result, rng, source, target, shards_of, factor):
    owner, partner = [(jnp.arange(result.shape[axis_at]) // (result.shape[axis_at] // shards_of)).reshape([-1 if axis == axis_at else 1 for axis in range(result.ndim)]) for axis_at in (source, target)]
    chosen = jax.random.permutation(rng, shards_of)[partner]
    strong = (owner == chosen) | (owner == (partner + shards_of // 2) % shards_of)
    return jnp.where(strong, factor * result, result)


def steps_of(stream_key, shape, shards, least, high):
    def one(dim, blocks):
        draws = jax.random.uniform(jax.random.fold_in(jax.random.fold_in(stream_key, 6), dim), (blocks,), jnp.float32, least / len(shards), high / len(shards))
        return jnp.repeat(jnp.exp(draws), shape[dim] // blocks).reshape((-1,) + (1,) * (len(shape) - dim - 1))

    gain = one(*shards[0])
    for cut in shards[1:]:
        gain = gain * one(*cut)
    return gain


def gaussian(stream_key, extent, spread, reach, shards=(), held_as=jnp.bfloat16):
    factor_of = steps_of(stream_key, extent, shards, -0.22, 0.18) if shards else 1.0
    entries = jax.random.normal(stream_key, extent, jnp.float32) * spread * factor_of
    return jnp.minimum(jnp.maximum(entries, -reach), reach).astype(held_as)


def heavy_noise(key, shape, width, most, shards, heavy, kind=jnp.bfloat16):
    values = width * jax.random.normal(key, shape, jnp.float32)
    if shards:
        values = values * steps_of(key, shape, shards, -0.22, 0.18)
    return jnp.clip(with_spikes(values, jax.random.fold_in(key, 3), *heavy), -most, most).astype(kind)


def setup_inputs(seed: int = 0) -> dict:
    splits = jax.random.split(jax.random.key(seed), 5)
    return {
        "integrals": heavy_noise(splits[0], (NPAIR, 2, NAUX, NORB, NORB), 1.0, 6.0, ((0, 16), (2, 8)), (2, 3, 8, 2.0)),
        "coef_table": gaussian(splits[1], (NKPT * NORB, 2, NOCC), NORB ** -0.5, 0.375, ((0, 16),)),
        "row_slot": jax.random.permutation(splits[2], NKPT * NORB).astype(jnp.int32),
        "pair_k": draw_pair_k(jax.random.fold_in(splits[4], 71), 0),
    }


def pick_rows(coef_table, row_slot, kpoint):
    slots = lax.dynamic_slice_in_dim(row_slot, (kpoint * NORB).astype(jnp.int32), NORB)
    return coef_table[slots].reshape(NORB, 2 * NOCC).astype(jnp.float32)


def exchange_block(real_part, imag_part):
    rounded_real = lax.optimization_barrier(real_part.astype(jnp.bfloat16)).astype(jnp.float32)
    rounded_imag = lax.optimization_barrier(imag_part.astype(jnp.bfloat16)).astype(jnp.float32)
    joined = jnp.concatenate([rounded_real, rounded_imag], -1)
    turned = jnp.concatenate([rounded_imag, -rounded_real], -1)
    k_real = jnp.einsum("pmj,plj->ml", joined, joined)
    k_imag = jnp.einsum("pmj,plj->ml", turned, joined)
    return jnp.stack([k_real, k_imag]) / (NAUX * NOCC)


def reference(integrals, coef_table, row_slot, pair_k):
    kpoints = jnp.arange(NKPT, dtype=jnp.int32)

    def step(total, inputs):
        blocks, kpair = inputs
        blocks = blocks.astype(jnp.float32)
        first_k = kpair[0]
        second_k = kpair[1]
        coeff_second = pick_rows(coef_table, row_slot, second_k)
        coeff_first = pick_rows(coef_table, row_slot, first_k)
        product = jnp.einsum("cpmn,nj->cpmj", blocks, coeff_second)
        left_real = product[0, ..., :NOCC] - product[1, ..., NOCC:]
        left_imag = product[0, ..., NOCC:] + product[1, ..., :NOCC]
        first_block = exchange_block(left_real, left_imag)
        product = jnp.einsum("cpmn,mj->cpnj", blocks, coeff_first)
        right_real = product[0, ..., :NOCC] + product[1, ..., NOCC:]
        right_imag = product[0, ..., NOCC:] - product[1, ..., :NOCC]
        second_block = exchange_block(right_real, right_imag)
        first_hot = (kpoints == first_k).astype(jnp.float32)[None, :, None, None]
        second_hot = (kpoints == second_k).astype(jnp.float32)[None, :, None, None]
        total = total + first_block[:, None] * first_hot + second_block[:, None] * second_hot
        return total, None

    start = jnp.zeros((2, NKPT, NORB, NORB), jnp.float32)
    total, unused = lax.scan(step, start, (integrals, pair_k))
    return total
```

```python
import jax
import jax.numpy as jnp
from jax import lax
from jax.experimental import pallas as pl
from jax.experimental.pallas import tpu as pltpu
from jax.sharding import PartitionSpec as P

NKPT = 8
NORB = 256
NOCC = 128
NPAIR = 16
NSLAB = 8
ROWS = 128
PIECE = 144
GROUP = 16
CHUNKS = 16
F32 = jnp.float32
BF16 = jnp.bfloat16
MESH = pl.DeviceIdType.MESH


def product(left, right):
    return lax.dot_general(left, right, (((1,), (0,)), ((), ())), preferred_element_type=F32)


def product_nt(left, right):
    return lax.dot_general(left, right, (((1,), (1,)), ((), ())), preferred_element_type=F32)


def product_tn(left, right):
    return lax.dot_general(left, right, (((0,), (0,)), ((), ())), preferred_element_type=F32)


def kernel(pair_ref, piece_ref, slot_ref, blocks_ref, out_ref, blocks, table, picked, first_w, second_w,
           k_real, k_cross, sums_out, sums_in, tiles_out, tiles_in,
           load_sem, table_send, table_recv, sums_send, sums_recv, tiles_send, tiles_recv):
    me = lax.axis_index("pair")
    slab = lax.axis_index("aux")
    naux = blocks.shape[1]
    step = naux // CHUNKS
    factor = 1.0 / (naux * NSLAB * NOCC)

    def load(chunk):
        span = pl.ds(chunk * step, step)
        return pltpu.make_async_copy(blocks_ref.at[:, span], blocks.at[:, span], load_sem.at[chunk])

    for chunk in range(CHUNKS):
        load(chunk).start()

    barrier = pltpu.get_barrier_semaphore()
    for offset in range(1, NPAIR):
        pl.semaphore_signal(barrier, inc=1, device_id=(lax.rem(me + offset, NPAIR), slab), device_id_type=MESH)
    for offset in range(1, NSLAB):
        pl.semaphore_signal(barrier, inc=1, device_id=(me, lax.rem(slab + offset, NSLAB)), device_id_type=MESH)

    first_k = pair_ref[0, 0]
    second_k = pair_ref[0, 1]
    slots = slot_ref[...]
    columns = []
    for kpoint in (second_k, first_k):
        for half in range(2):
            row = jnp.zeros((1, ROWS), jnp.int32)
            for k in range(NKPT):
                row = jnp.where(kpoint == k, slots[2 * k + half:2 * k + half + 1], row)
            columns.append(jnp.broadcast_to(row, (ROWS, ROWS)).T)
    wanted = jnp.concatenate(columns, 0)
    lane = lax.broadcasted_iota(jnp.int32, wanted.shape, 1)

    pl.semaphore_wait(barrier, NPAIR + NSLAB - 2)

    def table_copy(offset):
        return pltpu.make_async_remote_copy(
            src_ref=piece_ref, dst_ref=table.at[me], send_sem=table_send.at[offset], recv_sem=table_recv.at[offset],
            device_id=(lax.rem(me + offset, NPAIR), slab), device_id_type=MESH)

    for offset in range(1, NPAIR):
        table_copy(offset).start()
    table[me] = piece_ref[...]

    for offset in range(NPAIR):
        owner = lax.rem(me + NPAIR - offset, NPAIR)
        if offset:
            table_copy(offset).wait_recv()
        hot = jnp.where(wanted == owner * ROWS + lane, 1.0, 0.0).astype(BF16)
        term = product(hot, table[owner, :ROWS])
        if offset:
            picked[...] += term
        else:
            picked[...] = term

    for at, ref in ((0, second_w), (NORB, first_w)):
        real = picked[at:at + NORB, :NOCC]
        imag = picked[at:at + NORB, NOCC:]
        if ref is second_w:
            ref[...] = jnp.concatenate(
                [jnp.concatenate([real, imag], 1), jnp.concatenate([-imag, real], 1)], 0).astype(BF16)
        else:
            ref[...] = jnp.concatenate(
                [jnp.concatenate([real, imag], 1).T, jnp.concatenate([imag, -real], 1).T], 1).astype(BF16)

    def sums_copy(block, offset):
        peer = lax.rem(slab + offset, NSLAB)
        return pltpu.make_async_remote_copy(
            src_ref=sums_out.at[block, peer], dst_ref=sums_in.at[block, slab],
            send_sem=sums_send.at[block, offset], recv_sem=sums_recv.at[block, offset],
            device_id=(me, peer), device_id_type=MESH)

    def clear():
        k_real[...] = jnp.zeros_like(k_real)
        k_cross[...] = jnp.zeros_like(k_cross)

    def send_sums(block):
        cross = k_cross[...]
        parts = (k_real[...] * factor, (cross.T - cross) * factor)
        at = lax.broadcasted_iota(jnp.int32, (ROWS, ROWS), 1)
        for peer in range(NSLAB):
            tile, shift = peer // 4, peer % 4 * 32
            message = None
            for half in range(2):
                for part in range(2):
                    begin = half * 64 + part * 32
                    value = parts[part][half * ROWS:(half + 1) * ROWS, tile * ROWS:(tile + 1) * ROWS]
                    turn = (begin - shift) % ROWS
                    if turn:
                        value = pltpu.roll(value, turn, 1)
                    message = value if message is None else jnp.where(at >= begin, value, message)
            sums_out[block, peer] = message
        for offset in range(1, NSLAB):
            sums_copy(block, offset).start()

    clear()

    def left(group, carry):
        for chunk in range(GROUP // step):
            load(group * (GROUP // step) + chunk).wait()
        rounded = []
        for p in range(GROUP):
            both = jnp.concatenate([blocks[0, group * GROUP + p], blocks[1, group * GROUP + p]], 1)
            rounded.append(product(both, second_w[...]).astype(BF16))
        real = jnp.concatenate([x[:, :NOCC] for x in rounded], 1)
        imag = jnp.concatenate([x[:, NOCC:] for x in rounded], 1)
        terms = product_nt(jnp.concatenate([real, imag], 0), real)
        k_real[...] += terms[:NORB] + product_nt(imag, imag)
        k_cross[...] += terms[NORB:]
        return carry

    lax.fori_loop(0, naux // GROUP, left, 0)
    send_sums(0)
    clear()

    def right(group, carry):
        rounded = []
        for p in range(GROUP):
            both = jnp.concatenate([blocks[0, group * GROUP + p], blocks[1, group * GROUP + p]], 0)
            rounded.append(product(first_w[...], both).astype(BF16))
        real = jnp.concatenate([x[:NOCC] for x in rounded], 0)
        imag = jnp.concatenate([x[NOCC:] for x in rounded], 0)
        terms = product_tn(jnp.concatenate([real, imag], 1), real)
        k_real[...] += terms[:NORB] + product_tn(imag, imag)
        k_cross[...] += terms[NORB:]
        return carry

    lax.fori_loop(0, naux // GROUP, right, 0)
    send_sums(1)

    low = lax.broadcasted_iota(jnp.int32, (ROWS, ROWS), 1) < 64
    totals = []
    for block in range(2):
        sums_in[block, slab] = sums_out[block, slab]
        for offset in range(1, NSLAB):
            sums_copy(block, offset).wait_recv()
        total = sums_in[block, 0]
        for sender in range(1, NSLAB):
            total = total + sums_in[block, sender]
        totals.append(total)
    tiles_out[:ROWS] = jnp.where(low, totals[0], pltpu.roll(totals[1], 64, 1))
    tiles_out[ROWS:] = jnp.where(low, pltpu.roll(totals[0], 64, 1), totals[1])

    def tile_copy(offset):
        peer = lax.rem(me + offset, NPAIR)
        return pltpu.make_async_remote_copy(
            src_ref=tiles_out.at[pl.ds(pl.multiple_of(peer * 16, 16), 16)], dst_ref=tiles_in.at[me],
            send_sem=tiles_send.at[offset], recv_sem=tiles_recv.at[offset],
            device_id=(peer, slab), device_id_type=MESH)

    for offset in range(1, NPAIR):
        tile_copy(offset).start()
    tiles_in[me] = tiles_out[pl.ds(pl.multiple_of(me * 16, 16), 16)]
    for offset in range(1, NPAIR):
        tile_copy(offset).wait_recv()
    kept = [jnp.zeros((16, ROWS), F32) for k in range(NKPT)]
    for owner in range(NPAIR):
        kpoint = table[owner, ROWS:PIECE, :ROWS].astype(F32)
        tile = tiles_in[owner]
        kept = [kept[k] + jnp.where(kpoint == k, tile, 0.0) for k in range(NKPT)]
    kept = [value + pltpu.roll(value, 64, 1) for value in kept]
    out_ref[...] = jnp.concatenate(kept, 0).T[:64]

    for offset in range(1, NPAIR):
        table_copy(offset).wait_send()
        tile_copy(offset).wait_send()
    for offset in range(1, NSLAB):
        sums_copy(0, offset).wait_send()
        sums_copy(1, offset).wait_send()


def local(integrals, coef_table, row_slot, pair_k):
    naux = integrals.shape[2]
    blocks = integrals.reshape(integrals.shape[1:])
    kpoints = jnp.repeat(pair_k.astype(BF16), 64, axis=1)
    kpoints = jnp.broadcast_to(jnp.concatenate([kpoints, kpoints], 1), (PIECE - ROWS, NORB))
    piece = jnp.concatenate([coef_table.reshape(ROWS, 2 * NOCC), kpoints], 0)
    vmem = pl.BlockSpec(memory_space=pltpu.VMEM)
    out = pl.pallas_call(
        kernel,
        out_shape=jax.ShapeDtypeStruct((64, ROWS), F32),
        in_specs=[pl.BlockSpec(memory_space=pltpu.SMEM), vmem, vmem, pl.BlockSpec(memory_space=pl.ANY)],
        out_specs=vmem,
        scratch_shapes=[
            pltpu.VMEM((2, naux, NORB, NORB), BF16),
            pltpu.VMEM((NPAIR, PIECE, NORB), BF16),
            pltpu.VMEM((2 * NORB, NORB), F32),
            pltpu.VMEM((NORB, 2 * NORB), BF16),
            pltpu.VMEM((2 * NORB, NORB), BF16),
            pltpu.VMEM((NORB, NORB), F32),
            pltpu.VMEM((NORB, NORB), F32),
            pltpu.VMEM((2, NSLAB, ROWS, ROWS), F32),
            pltpu.VMEM((2, NSLAB, ROWS, ROWS), F32),
            pltpu.VMEM((NORB, ROWS), F32),
            pltpu.VMEM((NPAIR, 16, ROWS), F32),
            pltpu.SemaphoreType.DMA((CHUNKS,)),
            pltpu.SemaphoreType.DMA((NPAIR,)),
            pltpu.SemaphoreType.DMA((NPAIR,)),
            pltpu.SemaphoreType.DMA((2, NSLAB)),
            pltpu.SemaphoreType.DMA((2, NSLAB)),
            pltpu.SemaphoreType.DMA((NPAIR,)),
            pltpu.SemaphoreType.DMA((NPAIR,)),
        ],
        compiler_params=pltpu.CompilerParams(
            collective_id=0, has_side_effects=True, vmem_limit_bytes=56 * 2**20),
    )(pair_k, piece, row_slot.reshape(16, ROWS), blocks)
    return out.reshape(2, 32, NKPT, 16).transpose(0, 2, 1, 3)


def solution(mesh):
    in_specs = (P("pair", None, "aux", None, None), P("pair", None, None), P(), P("pair", None))
    out_specs = P(None, None, "aux", "pair")
    return jax.shard_map(local, mesh=mesh, in_specs=in_specs, out_specs=out_specs, check_vma=False)
```

```python
import jax
import jax.numpy as jnp
from jax import lax
from jax.experimental import pallas as pl
from jax.experimental.pallas import tpu as pltpu
from jax.sharding import PartitionSpec as P

NKPT = 8
NORB = 256
NOCC = 128
NPAIR = 16
NSLAB = 8
ROWS = 128
HALVES = 2
GROUP = 16
CHUNKS = 16
F32 = jnp.float32
BF16 = jnp.bfloat16
MESH = pl.DeviceIdType.MESH


def product(left, right):
    return lax.dot_general(left, right, (((1,), (0,)), ((), ())), preferred_element_type=F32)


def product_nt(left, right):
    return lax.dot_general(left, right, (((1,), (1,)), ((), ())), preferred_element_type=F32)


def product_tn(left, right):
    return lax.dot_general(left, right, (((0,), (0,)), ((), ())), preferred_element_type=F32)


def neighbours(me, slab):
    x, low, core = me // 4, me // 2 % 2, me % 2
    y, high = slab // 2, slab % 2
    across = x * 4 + (1 - low) * 2 + core
    return {
        "x+": (lax.rem(x + 1, 4) * 4 + low * 2 + core, slab),
        "x-": (lax.rem(x + 3, 4) * 4 + low * 2 + core, slab),
        "z+": (across, y * 2 + lax.rem(high + low, 2)),
        "z-": (across, y * 2 + lax.rem(high + 1 - low, 2)),
        "core": (me + 1 - 2 * core, slab),
    }


def kernel(pair_ref, piece_ref, slot_ref, blocks_ref, out_ref, blocks, table, offsets, picked, first_w, second_w,
           k_real, k_cross, sums_out, sums_in, tiles_out, tiles_in,
           load_sem, table_send, table_recv, sums_send, sums_recv, tiles_send, tiles_recv):
    me = lax.axis_index("pair")
    slab = lax.axis_index("aux")
    naux = blocks.shape[1]
    step = naux // CHUNKS
    factor = 1.0 / (naux * NSLAB * NOCC)
    peers = neighbours(me, slab)

    def load(chunk):
        span = pl.ds(chunk * step, step)
        return pltpu.make_async_copy(blocks_ref.at[:, span], blocks.at[:, span], load_sem.at[chunk])

    barrier = pltpu.get_barrier_semaphore()
    greeted = [peers["z+"], peers["z-"]]
    greeted += [(lax.rem(me + offset, NPAIR), slab) for offset in range(1, NPAIR)]
    greeted += [(me, lax.rem(slab + offset, NSLAB)) for offset in range(1, NSLAB)]
    for peer in greeted:
        pl.semaphore_signal(barrier, inc=1, device_id=peer, device_id_type=MESH)

    for chunk in range(CHUNKS):
        load(chunk).start()

    first_k = pair_ref[0, 0]
    second_k = pair_ref[0, 1]
    slots = slot_ref[...]
    lane = lax.broadcasted_iota(jnp.int32, (ROWS, ROWS), 1)
    for at, kpoint in enumerate((second_k, first_k)):
        for half in range(2):
            row = jnp.zeros((1, ROWS), jnp.int32)
            for k in range(NKPT):
                row = jnp.where(kpoint == k, slots[2 * k + half:2 * k + half + 1], row)
            place = 2 * jnp.broadcast_to(row, (ROWS, ROWS)).T - lane
            for part in range(2):
                begin = (at * 4 + part * 2 + half) * ROWS
                offsets[begin:begin + ROWS] = place + part

    pl.semaphore_wait(barrier, len(greeted))

    low_z, core = me // 2 % 2, me % 2
    x = me // 4
    own = {(dx, dz): lax.rem(x + dx, 4) * 4 + (low_z if dz == 0 else 1 - low_z) * 2 + core
           for dx in range(4) for dz in range(2)}
    lanes_of = {}

    def table_copy(source, half, peer):
        key = (source, half, peer)
        at = lanes_of.setdefault(key, len(lanes_of))
        slot = own[source]
        origin = piece_ref.at[half] if source == (0, 0) else table.at[slot, half]
        return pltpu.make_async_remote_copy(
            src_ref=origin, dst_ref=table.at[slot, half], send_sem=table_send.at[at], recv_sem=table_recv.at[at],
            device_id=peers[peer], device_id_type=MESH)

    sent = []

    def send(source, half, peer):
        copy = table_copy(source, half, peer)
        copy.start()
        sent.append(copy)

    def arrive(source, half, peer):
        dx, dz = source
        if peer[0] == "x":
            dx = (dx + (1 if peer == "x+" else 3)) % 4
        if peer[0] == "z":
            dz = 1 - dz
        table_copy((dx, dz), half, peer).wait_recv()

    def pick(slot, source=None):
        rows = table[slot].reshape(2 * ROWS, ROWS) if source is None else source
        base = slot * (2 * ROWS)
        hot = [jnp.where(offsets[...] == base + half * ROWS, 1.0, 0.0).astype(BF16) for half in range(HALVES)]
        return product(jnp.concatenate(hot, 1), rows)

    def other(slot):
        return slot + 1 - 2 * core

    def from_core(source):
        for half in range(HALVES):
            at = lanes_of[(source, half, "core")]
            slot = other(own[source])
            pltpu.make_async_remote_copy(
                src_ref=table.at[slot, half], dst_ref=table.at[slot, half],
                send_sem=table_send.at[at], recv_sem=table_recv.at[at],
                device_id=peers["core"], device_id_type=MESH).wait_recv()

    HERE, LEFT, RIGHT, FAR = (0, 0), (3, 0), (1, 0), (2, 0)
    send(HERE, 0, "x+")
    send(HERE, 1, "x-")
    send(HERE, 0, "z+")
    send(HERE, 1, "z-")
    send(HERE, 1, "x+")
    send(HERE, 0, "x-")
    send(HERE, 0, "core")
    send(HERE, 1, "core")
    picked[...] = pick(me, piece_ref[...].reshape(2 * ROWS, ROWS))
    arrive(LEFT, 0, "x+")
    send(LEFT, 0, "x+")
    send(LEFT, 0, "z+")
    send(LEFT, 0, "core")
    arrive(RIGHT, 1, "x-")
    send(RIGHT, 1, "x-")
    send(RIGHT, 1, "z-")
    send(RIGHT, 1, "core")
    arrive((0, 1), 0, "z+")
    send((0, 1), 0, "core")
    arrive((0, 1), 1, "z-")
    send((0, 1), 1, "core")
    arrive(LEFT, 1, "x+")
    send(LEFT, 1, "z+")
    send(LEFT, 1, "core")
    arrive(RIGHT, 0, "x-")
    send(RIGHT, 0, "z-")
    send(RIGHT, 0, "core")
    for source in (LEFT, RIGHT, (0, 1)):
        picked[...] += pick(own[source])
    from_core(HERE)
    picked[...] += pick(other(me))
    arrive(FAR, 0, "x+")
    send(FAR, 0, "z+")
    send(FAR, 0, "core")
    arrive(FAR, 1, "x-")
    send(FAR, 1, "z-")
    send(FAR, 1, "core")
    picked[...] += pick(own[FAR])
    for source, peer in (((3, 1), "z+"), ((1, 1), "z-")):
        for half in range(HALVES):
            arrive(source, half, peer)
            send(source, half, "core")
        picked[...] += pick(own[source])
    for source in (LEFT, RIGHT, (0, 1), FAR):
        from_core(source)
        picked[...] += pick(other(own[source]))
    arrive((2, 1), 0, "z+")
    send((2, 1), 0, "core")
    arrive((2, 1), 1, "z-")
    send((2, 1), 1, "core")
    for source in ((3, 1), (1, 1)):
        from_core(source)
        picked[...] += pick(other(own[source]))
    picked[...] += pick(own[(2, 1)])
    from_core((2, 1))
    picked[...] += pick(other(own[(2, 1)]))

    parts = [picked[begin:begin + NORB] for begin in range(0, 4 * NORB, NORB)]
    real, imag = parts[:2]
    second_w[...] = jnp.concatenate(
        [jnp.concatenate([real, imag], 1), jnp.concatenate([-imag, real], 1)], 0).astype(BF16)
    real, imag = parts[2:]
    first_w[...] = jnp.concatenate(
        [jnp.concatenate([real, imag], 1).T, jnp.concatenate([imag, -real], 1).T], 1).astype(BF16)

    def sums_copy(block, offset):
        peer = lax.rem(slab + offset, NSLAB)
        return pltpu.make_async_remote_copy(
            src_ref=sums_out.at[block, peer], dst_ref=sums_in.at[block, slab],
            send_sem=sums_send.at[block, offset], recv_sem=sums_recv.at[block, offset],
            device_id=(me, peer), device_id_type=MESH)

    def clear():
        k_real[...] = jnp.zeros_like(k_real)
        k_cross[...] = jnp.zeros_like(k_cross)

    def send_sums(block):
        cross = k_cross[...]
        parts = (k_real[...] * factor, (cross.T - cross) * factor)
        at = lax.broadcasted_iota(jnp.int32, (ROWS, ROWS), 1)
        for peer in range(NSLAB):
            tile, shift = peer // 4, peer % 4 * 32
            message = None
            for half in range(2):
                for part in range(2):
                    begin = half * 64 + part * 32
                    value = parts[part][half * ROWS:(half + 1) * ROWS, tile * ROWS:(tile + 1) * ROWS]
                    turn = (begin - shift) % ROWS
                    if turn:
                        value = pltpu.roll(value, turn, 1)
                    message = value if message is None else jnp.where(at >= begin, value, message)
            sums_out[block, peer] = message
        for offset in range(1, NSLAB):
            sums_copy(block, offset).start()

    clear()

    def left(group, carry):
        for chunk in range(GROUP // step):
            load(group * (GROUP // step) + chunk).wait()
        rounded = []
        for p in range(GROUP):
            both = jnp.concatenate([blocks[0, group * GROUP + p], blocks[1, group * GROUP + p]], 1)
            rounded.append(product(both, second_w[...]).astype(BF16))
        real = jnp.concatenate([x[:, :NOCC] for x in rounded], 1)
        imag = jnp.concatenate([x[:, NOCC:] for x in rounded], 1)
        terms = product_nt(jnp.concatenate([real, imag], 0), real)
        k_real[...] += terms[:NORB] + product_nt(imag, imag)
        k_cross[...] += terms[NORB:]
        return carry

    lax.fori_loop(0, naux // GROUP, left, 0)
    send_sums(0)
    clear()

    def right(group, carry):
        rounded = []
        for p in range(GROUP):
            both = jnp.concatenate([blocks[0, group * GROUP + p], blocks[1, group * GROUP + p]], 0)
            rounded.append(product(first_w[...], both).astype(BF16))
        real = jnp.concatenate([x[:NOCC] for x in rounded], 0)
        imag = jnp.concatenate([x[NOCC:] for x in rounded], 0)
        terms = product_tn(jnp.concatenate([real, imag], 1), real)
        k_real[...] += terms[:NORB] + product_tn(imag, imag)
        k_cross[...] += terms[NORB:]
        return carry

    lax.fori_loop(0, naux // GROUP, right, 0)
    send_sums(1)

    low = lax.broadcasted_iota(jnp.int32, (ROWS, ROWS), 1) < 64
    tiles_out[:, 16:] = jnp.broadcast_to(
        jnp.where(low[:1], first_k, second_k).astype(F32), (NPAIR, 8, ROWS))
    totals = []
    for block in range(2):
        sums_in[block, slab] = sums_out[block, slab]
        for offset in range(1, NSLAB):
            sums_copy(block, offset).wait_recv()
        total = sums_in[block, 0]
        for sender in range(1, NSLAB):
            total = total + sums_in[block, sender]
        totals.append(total)
    tiles_out[:8, :16] = jnp.where(low, totals[0], pltpu.roll(totals[1], 64, 1)).reshape(8, 16, ROWS)
    tiles_out[8:, :16] = jnp.where(low, pltpu.roll(totals[0], 64, 1), totals[1]).reshape(8, 16, ROWS)

    def tile_copy(offset):
        peer = lax.rem(me + offset, NPAIR)
        return pltpu.make_async_remote_copy(
            src_ref=tiles_out.at[peer], dst_ref=tiles_in.at[me],
            send_sem=tiles_send.at[offset], recv_sem=tiles_recv.at[offset],
            device_id=(peer, slab), device_id_type=MESH)

    for offset in range(1, NPAIR):
        tile_copy(offset).start()
    tiles_in[me] = tiles_out[me]
    for offset in range(1, NPAIR):
        tile_copy(offset).wait_recv()
    kept = [jnp.zeros((16, ROWS), F32) for k in range(NKPT)]
    for owner in range(NPAIR):
        tile = tiles_in[owner, :16]
        kpoint = tiles_in[owner, 16:17]
        kept = [kept[k] + jnp.where(kpoint == k, tile, 0.0) for k in range(NKPT)]
    for k in range(NKPT):
        value = kept[k] + pltpu.roll(kept[k], 64, 1)
        out_ref[0, k] = value[:, :32]
        out_ref[1, k] = value[:, 32:64]

    for copy in sent:
        copy.wait_send()
    for offset in range(1, NPAIR):
        tile_copy(offset).wait_send()
    for offset in range(1, NSLAB):
        sums_copy(0, offset).wait_send()
        sums_copy(1, offset).wait_send()


def local(integrals, coef_table, row_slot, pair_k):
    naux = integrals.shape[2]
    blocks = integrals.reshape(integrals.shape[1:])
    vmem = pl.BlockSpec(memory_space=pltpu.VMEM)
    out = pl.pallas_call(
        kernel,
        out_shape=jax.ShapeDtypeStruct((2, NKPT, 16, 32), F32),
        in_specs=[pl.BlockSpec(memory_space=pltpu.SMEM), vmem, vmem, pl.BlockSpec(memory_space=pl.ANY)],
        out_specs=vmem,
        scratch_shapes=[
            pltpu.VMEM((2, naux, NORB, NORB), BF16),
            pltpu.VMEM((NPAIR, HALVES, ROWS, ROWS), BF16),
            pltpu.VMEM((4 * NORB, ROWS), jnp.int32),
            pltpu.VMEM((4 * NORB, ROWS), F32),
            pltpu.VMEM((NORB, 2 * NORB), BF16),
            pltpu.VMEM((2 * NORB, NORB), BF16),
            pltpu.VMEM((NORB, NORB), F32),
            pltpu.VMEM((NORB, NORB), F32),
            pltpu.VMEM((2, NSLAB, ROWS, ROWS), F32),
            pltpu.VMEM((2, NSLAB, ROWS, ROWS), F32),
            pltpu.VMEM((NPAIR, 24, ROWS), F32),
            pltpu.VMEM((NPAIR, 24, ROWS), F32),
            pltpu.SemaphoreType.DMA((CHUNKS,)),
            pltpu.SemaphoreType.DMA((30,)),
            pltpu.SemaphoreType.DMA((30,)),
            pltpu.SemaphoreType.DMA((2, NSLAB)),
            pltpu.SemaphoreType.DMA((2, NSLAB)),
            pltpu.SemaphoreType.DMA((NPAIR,)),
            pltpu.SemaphoreType.DMA((NPAIR,)),
        ],
        compiler_params=pltpu.CompilerParams(
            collective_id=0, has_side_effects=True, vmem_limit_bytes=56 * 2**20),
    )(pair_k, coef_table.reshape(HALVES, ROWS, ROWS), row_slot.reshape(16, ROWS), blocks)
    return out.transpose(0, 1, 3, 2)


def solution(mesh):
    in_specs = (P("pair", None, "aux", None, None), P("pair", None, None), P(), P("pair", None))
    out_specs = P(None, None, "aux", "pair")
    return jax.shard_map(local, mesh=mesh, in_specs=in_specs, out_specs=out_specs, check_vma=False)
```

```python
import jax
import jax.numpy as jnp
from jax import lax
from jax.experimental import pallas as pl
from jax.experimental.pallas import tpu as pltpu
from jax.sharding import PartitionSpec as P

NKPT = 8
NORB = 256
NOCC = 128
NPAIR = 16
NSLAB = 8
ROWS = 128
HALVES = 2
GROUP = 16
CHUNKS = 16
F32 = jnp.float32
BF16 = jnp.bfloat16
MESH = pl.DeviceIdType.MESH


def product(left, right):
    return lax.dot_general(left, right, (((1,), (0,)), ((), ())), preferred_element_type=F32)


def product_nt(left, right):
    return lax.dot_general(left, right, (((1,), (1,)), ((), ())), preferred_element_type=F32)


def product_tn(left, right):
    return lax.dot_general(left, right, (((0,), (0,)), ((), ())), preferred_element_type=F32)


def places(me, slab):
    x, low, core = me // 4, me // 2 % 2, me % 2
    y, high = slab // 2, slab % 2
    beyond = (y * 2 + lax.rem(high + low, 2), y * 2 + lax.rem(high + 1 - low, 2))

    def place(dx, dz=0, way=0):
        pair = lax.rem(x + dx, 4) * 4 + (1 - low if dz else low) * 2 + core
        return pair, (beyond[way] if dz else slab)

    return place


def kernel(pair_hbm, piece_hbm, slot_hbm, blocks_ref, out_ref, pair_ref, slot_ref, blocks, table, offsets, picked,
           second_w, first_w, kept, kept_turned, k_real, k_cross, sums_out, sums_in, tiles_out, tiles_in,
           load_sem, table_send, table_recv, sums_send, sums_recv, tiles_send, tiles_recv):
    me = lax.axis_index("pair")
    slab = lax.axis_index("aux")
    naux = blocks.shape[1]
    step = naux // CHUNKS
    factor = 1.0 / (naux * NSLAB * NOCC)
    place = places(me, slab)
    core = me % 2
    partner = (me + 1 - 2 * core, slab)

    def load(chunk):
        span = pl.ds(chunk * step, step)
        return pltpu.make_async_copy(blocks_ref.at[:, span], blocks.at[:, span], load_sem.at[chunk])

    barrier = pltpu.get_barrier_semaphore()
    beyond = (slab // 2) * 2 + 1 - slab % 2
    greeted = [(place(dx, 1)[0], beyond) for dx in range(4)]
    greeted += [(lax.rem(me + offset, NPAIR), slab) for offset in range(1, NPAIR)]
    greeted += [(me, lax.rem(slab + offset, NSLAB)) for offset in range(1, NSLAB)]
    for peer in greeted:
        pl.semaphore_signal(barrier, inc=1, device_id=peer, device_id_type=MESH)

    small = [pltpu.make_async_copy(pair_hbm, pair_ref, load_sem.at[CHUNKS]),
             pltpu.make_async_copy(slot_hbm, slot_ref, load_sem.at[CHUNKS + 1]),
             pltpu.make_async_copy(piece_hbm, table.at[me], load_sem.at[CHUNKS + 2])]
    for copy in small:
        copy.start()
    for copy in small:
        copy.wait()

    first_k = pair_ref[0, 0]
    second_k = pair_ref[0, 1]
    slots = slot_ref[...]
    lane = lax.broadcasted_iota(jnp.int32, (ROWS, ROWS), 1)
    for at, kpoint in enumerate((second_k, first_k)):
        for half in range(2):
            row = jnp.zeros((1, ROWS), jnp.int32)
            for k in range(NKPT):
                row = jnp.where(kpoint == k, slots[2 * k + half:2 * k + half + 1], row)
            where = 2 * jnp.broadcast_to(row, (ROWS, ROWS)).T - lane
            for part in range(2):
                begin = (at * 4 + part * 2 + half) * ROWS
                offsets[begin:begin + ROWS] = where + part

    pl.semaphore_wait(barrier, len(greeted))

    sources = [(0, 1), (1, 0), (3, 0), (1, 1), (3, 1), (2, 0), (2, 1)]

    def owner_of(dx, dz):
        return place(4 - dx, dz)[0]

    def table_copy(source, half):
        at = sources.index(source) * HALVES + half
        return pltpu.make_async_remote_copy(
            src_ref=table.at[me, half], dst_ref=table.at[me, half],
            send_sem=table_send.at[at], recv_sem=table_recv.at[at],
            device_id=place(*source, half), device_id_type=MESH)

    def core_copy(source, half):
        at = (len(sources) if source is None else sources.index(source)) * HALVES + half + 14
        slot = me if source is None else owner_of(*source)
        return pltpu.make_async_remote_copy(
            src_ref=table.at[slot, half], dst_ref=table.at[slot, half],
            send_sem=table_send.at[at], recv_sem=table_recv.at[at],
            device_id=partner, device_id_type=MESH)

    def pick(slot):
        rows = table[slot].reshape(2 * ROWS, ROWS)
        base = slot * (2 * ROWS)
        hot = [jnp.where(offsets[...] == base + half * ROWS, 1.0, 0.0).astype(BF16) for half in range(HALVES)]
        return product(jnp.concatenate(hot, 1), rows)

    def other(slot):
        return slot + 1 - 2 * core

    for source in sources:
        for half in range(HALVES):
            table_copy(source, half).start()
    for half in range(HALVES):
        core_copy(None, half).start()
    for chunk in range(CHUNKS):
        load(chunk).start()
    picked[...] = pick(me)
    for half in range(HALVES):
        core_copy(None, half).wait_recv()
    picked[...] += pick(other(me))
    for source in sources:
        for half in range(HALVES):
            table_copy(source, half).wait_recv()
            core_copy(source, half).start()
        picked[...] += pick(owner_of(*source))
        at = sources.index(source)
        if at:
            for half in range(HALVES):
                core_copy(sources[at - 1], half).wait_recv()
            picked[...] += pick(other(owner_of(*sources[at - 1])))
    for half in range(HALVES):
        core_copy(sources[-1], half).wait_recv()
    picked[...] += pick(other(owner_of(*sources[-1])))

    parts = [picked[begin:begin + NORB] for begin in range(0, 4 * NORB, NORB)]
    real, imag = parts[:2]
    second_w[...] = jnp.concatenate(
        [jnp.concatenate([real, imag], 1), jnp.concatenate([-imag, real], 1)], 0).astype(BF16)
    real, imag = parts[2:]
    first_w[...] = jnp.concatenate(
        [jnp.concatenate([real, imag], 1).T, jnp.concatenate([imag, -real], 1).T], 1).astype(BF16)

    def sums_copy(block, part, offset):
        peer = lax.rem(slab + offset, NSLAB)
        return pltpu.make_async_remote_copy(
            src_ref=sums_out.at[block, part, peer], dst_ref=sums_in.at[block, part, slab],
            send_sem=sums_send.at[block, part, offset], recv_sem=sums_recv.at[block, part, offset],
            device_id=(me, peer), device_id_type=MESH)

    def clear():
        k_real[...] = jnp.zeros_like(k_real)
        k_cross[...] = jnp.zeros_like(k_cross)

    at = lax.broadcasted_iota(jnp.int32, (64, ROWS), 1)

    def send_sums(block, part):
        value = k_cross[...].T - k_cross[...] if part else k_real[...]
        value = (value * factor).reshape(8, 4, 8, NORB)
        for peer in range(NSLAB):
            tile, shift = peer // 4, peer % 4
            message = None
            for b in range(4):
                rows = value[:, b, :, tile * ROWS:(tile + 1) * ROWS].reshape(64, ROWS)
                turn = (b - shift) % 4 * 32
                if turn:
                    rows = pltpu.roll(rows, turn, 1)
                message = rows if message is None else jnp.where(at >= b * 32, rows, message)
            sums_out[block, part, peer] = message
        for offset in range(1, NSLAB):
            sums_copy(block, part, offset).start()

    clear()

    def left(group, carry):
        for chunk in range(GROUP // step):
            load(group * (GROUP // step) + chunk).wait()
        rounded = []
        for p in range(GROUP):
            both = jnp.concatenate([blocks[0, group * GROUP + p], blocks[1, group * GROUP + p]], 1)
            rounded.append(product(both, second_w[...]).astype(BF16))
        real = jnp.concatenate([x[:, :NOCC] for x in rounded], 1)
        imag = jnp.concatenate([x[:, NOCC:] for x in rounded], 1)
        terms = product_nt(jnp.concatenate([real, imag], 0), real)
        k_real[...] += terms[:NORB] + product_nt(imag, imag)
        k_cross[...] += terms[NORB:]
        return carry

    lax.fori_loop(0, naux // GROUP, left, 0)
    send_sums(0, 0)
    send_sums(0, 1)
    clear()

    def right(group, carry):
        rounded = []
        for p in range(GROUP):
            both = jnp.concatenate([blocks[0, group * GROUP + p], blocks[1, group * GROUP + p]], 0)
            rounded.append(product(first_w[...], both).astype(BF16))
        real = jnp.concatenate([x[:NOCC] for x in rounded], 0)
        imag = jnp.concatenate([x[NOCC:] for x in rounded], 0)
        turned = imag.T
        k_cross[...] += product(turned, real)
        kept[group, 0] = real
        kept[group, 1] = imag
        kept_turned[group, 0] = real.T
        kept_turned[group, 1] = turned
        return carry

    lax.fori_loop(0, naux // GROUP, right, 0)
    send_sums(1, 1)
    real = jnp.concatenate([kept[group, part] for group in range(naux // GROUP) for part in range(2)], 0)
    turned = jnp.concatenate([kept_turned[group, part] for group in range(naux // GROUP) for part in range(2)], 1)
    k_real[...] = product(turned, real)
    send_sums(1, 0)

    def total(block, part):
        sums_in[block, part, slab] = sums_out[block, part, slab]
        for offset in range(1, NSLAB):
            sums_copy(block, part, offset).wait_recv()
        value = sums_in[block, part, 0]
        for sender in range(1, NSLAB):
            value = value + sums_in[block, part, sender]
        return value

    def tile_copy(block, offset):
        peer = lax.rem(me + offset, NPAIR)
        begin, rows = (0, 16) if block == 0 else (16, 8)
        return pltpu.make_async_remote_copy(
            src_ref=tiles_out.at[peer, pl.ds(begin, rows)], dst_ref=tiles_in.at[me, pl.ds(begin, rows)],
            send_sem=tiles_send.at[block, offset], recv_sem=tiles_recv.at[block, offset],
            device_id=(peer, slab), device_id_type=MESH)

    low = at < 64
    row = lax.broadcasted_iota(jnp.int32, (8, ROWS), 0)
    tiles_out[:, 8:16] = jnp.broadcast_to(jnp.where(row == 0, first_k, second_k).astype(F32), (NPAIR, 8, ROWS))
    for block in range(2):
        parts = [None, None]
        for part in ((0, 1) if block == 0 else (1, 0)):
            parts[part] = total(block, part)
        real, imag = parts
        even = jnp.where(low, real, pltpu.roll(imag, 64, 1)).reshape(8, 8, ROWS)
        odd = jnp.where(low, pltpu.roll(real, 64, 1), imag).reshape(8, 8, ROWS)
        begin = block * 16
        for pair in range(NPAIR):
            tiles_out[pair, begin:begin + 8] = (odd if pair % 2 else even)[pair // 2]
        for offset in range(1, NPAIR):
            tile_copy(block, offset).start()
    tiles_in[me] = tiles_out[me]
    bins = [jnp.zeros((8, ROWS), F32) for k in range(NKPT)]
    for block in range(2):
        for offset in range(1, NPAIR):
            tile_copy(block, offset).wait_recv()
        for owner in range(NPAIR):
            tile = tiles_in[owner, block * 16:block * 16 + 8]
            kpoint = tiles_in[owner, 8 + block:9 + block]
            bins = [bins[k] + jnp.where(kpoint == k, tile, 0.0) for k in range(NKPT)]
    for k in range(NKPT):
        for part in range(2):
            for upper in range(2):
                begin = part * 64 + upper * 32
                out_ref[part, k, upper * 8:upper * 8 + 8] = bins[k][:, begin:begin + 32]

    for half in range(HALVES):
        core_copy(None, half).wait_send()
        for source in sources:
            table_copy(source, half).wait_send()
            core_copy(source, half).wait_send()
    for block in range(2):
        for offset in range(1, NPAIR):
            tile_copy(block, offset).wait_send()
        for part in range(2):
            for offset in range(1, NSLAB):
                sums_copy(block, part, offset).wait_send()


def local(integrals, coef_table, row_slot, pair_k):
    naux = integrals.shape[2]
    blocks = integrals.reshape(integrals.shape[1:])
    out = pl.pallas_call(
        kernel,
        out_shape=jax.ShapeDtypeStruct((2, NKPT, 16, 32), F32),
        in_specs=[pl.BlockSpec(memory_space=pl.ANY)] * 4,
        out_specs=pl.BlockSpec(memory_space=pltpu.VMEM),
        scratch_shapes=[
            pltpu.SMEM((1, 2), jnp.int32),
            pltpu.VMEM((16, ROWS), jnp.int32),
            pltpu.VMEM((2, naux, NORB, NORB), BF16),
            pltpu.VMEM((NPAIR, HALVES, ROWS, ROWS), BF16),
            pltpu.VMEM((4 * NORB, ROWS), jnp.int32),
            pltpu.VMEM((4 * NORB, ROWS), F32),
            pltpu.VMEM((2 * NORB, NORB), BF16),
            pltpu.VMEM((NORB, 2 * NORB), BF16),
            pltpu.VMEM((naux // GROUP, 2, GROUP * NOCC, NORB), BF16),
            pltpu.VMEM((naux // GROUP, 2, NORB, GROUP * NOCC), BF16),
            pltpu.VMEM((NORB, NORB), F32),
            pltpu.VMEM((NORB, NORB), F32),
            pltpu.VMEM((2, 2, NSLAB, 64, ROWS), F32),
            pltpu.VMEM((2, 2, NSLAB, 64, ROWS), F32),
            pltpu.VMEM((NPAIR, 24, ROWS), F32),
            pltpu.VMEM((NPAIR, 24, ROWS), F32),
            pltpu.SemaphoreType.DMA((CHUNKS + 3,)),
            pltpu.SemaphoreType.DMA((30,)),
            pltpu.SemaphoreType.DMA((30,)),
            pltpu.SemaphoreType.DMA((2, 2, NSLAB)),
            pltpu.SemaphoreType.DMA((2, 2, NSLAB)),
            pltpu.SemaphoreType.DMA((2, NPAIR)),
            pltpu.SemaphoreType.DMA((2, NPAIR)),
        ],
        compiler_params=pltpu.CompilerParams(
            collective_id=0, has_side_effects=True, vmem_limit_bytes=56 * 2**20),
    )(pair_k, coef_table.reshape(HALVES, ROWS, ROWS), row_slot.reshape(16, ROWS), blocks)
    return out.transpose(0, 1, 3, 2)


def solution(mesh):
    in_specs = (P("pair", None, "aux", None, None), P("pair", None, None), P(), P("pair", None))
    out_specs = P(None, None, "aux", "pair")
    return jax.shard_map(local, mesh=mesh, in_specs=in_specs, out_specs=out_specs, check_vma=False)
```

```python
import jax
import jax.numpy as jnp
from jax import lax
from jax.experimental import pallas as pl
from jax.experimental.pallas import tpu as pltpu
from jax.sharding import PartitionSpec as P

NKPT = 8
NORB = 256
NOCC = 128
NPAIR = 16
NSLAB = 8
ROWS = 128
HALVES = 2
GROUP = 16
CHUNKS = 16
F32 = jnp.float32
BF16 = jnp.bfloat16
MESH = pl.DeviceIdType.MESH
SUM_ORDER = ((2, 1), (1, 1), (3, 1), (2, 0), (0, 1), (1, 0), (3, 0))
TILE_ORDER = tuple((dx, dz, dc) for dx, dz in ((2, 1), (2, 0), (1, 1), (3, 1), (0, 1), (1, 0), (3, 0)) for dc in (0, 1)) + ((0, 0, 1),)


def product(left, right):
    return lax.dot_general(left, right, (((1,), (0,)), ((), ())), preferred_element_type=F32)


def product_nt(left, right):
    return lax.dot_general(left, right, (((1,), (1,)), ((), ())), preferred_element_type=F32)


def product_tn(left, right):
    return lax.dot_general(left, right, (((0,), (0,)), ((), ())), preferred_element_type=F32)


def places(me, slab):
    x, low, core = me // 4, me // 2 % 2, me % 2
    y, high = slab // 2, slab % 2
    beyond = (y * 2 + lax.rem(high + low, 2), y * 2 + lax.rem(high + 1 - low, 2))

    def place(dx, dz=0, way=0):
        pair = lax.rem(x + dx, 4) * 4 + (1 - low if dz else low) * 2 + core
        return pair, (beyond[way] if dz else slab)

    return place


def kernel(pair_hbm, piece_hbm, slot_hbm, blocks_ref, out_ref, pair_ref, slot_ref, blocks, table, offsets, picked,
           second_w, first_w, kept, kept_turned, k_real, k_cross, sums_out, sums_in, tiles_out, tiles_in,
           load_sem, table_send, table_recv, sums_send, sums_recv, tiles_send, tiles_recv):
    me = lax.axis_index("pair")
    slab = lax.axis_index("aux")
    naux = blocks.shape[1]
    step = naux // CHUNKS
    factor = 1.0 / (naux * NSLAB * NOCC)
    place = places(me, slab)
    core = me % 2
    partner = (me + 1 - 2 * core, slab)

    def load(chunk):
        span = pl.ds(chunk * step, step)
        return pltpu.make_async_copy(blocks_ref.at[:, span], blocks.at[:, span], load_sem.at[chunk])

    barrier = pltpu.get_barrier_semaphore()
    beyond = (slab // 2) * 2 + 1 - slab % 2
    greeted = [(place(dx, 1)[0], beyond) for dx in range(4)]
    greeted += [(lax.rem(me + offset, NPAIR), slab) for offset in range(1, NPAIR)]
    greeted += [(me, lax.rem(slab + offset, NSLAB)) for offset in range(1, NSLAB)]
    for peer in greeted:
        pl.semaphore_signal(barrier, inc=1, device_id=peer, device_id_type=MESH)

    small = [pltpu.make_async_copy(pair_hbm, pair_ref, load_sem.at[CHUNKS]),
             pltpu.make_async_copy(slot_hbm, slot_ref, load_sem.at[CHUNKS + 1]),
             pltpu.make_async_copy(piece_hbm, table.at[me], load_sem.at[CHUNKS + 2])]
    for copy in small:
        copy.start()
    for copy in small:
        copy.wait()

    first_k = pair_ref[0, 0]
    second_k = pair_ref[0, 1]
    slots = slot_ref[...]
    lane = lax.broadcasted_iota(jnp.int32, (ROWS, ROWS), 1)
    for at, kpoint in enumerate((second_k, first_k)):
        for half in range(2):
            row = jnp.zeros((1, ROWS), jnp.int32)
            for k in range(NKPT):
                row = jnp.where(kpoint == k, slots[2 * k + half:2 * k + half + 1], row)
            where = 2 * jnp.broadcast_to(row, (ROWS, ROWS)).T - lane
            for part in range(2):
                begin = (at * 4 + part * 2 + half) * ROWS
                offsets[begin:begin + ROWS] = where + part

    pl.semaphore_wait(barrier, len(greeted))

    sources = [(0, 1), (1, 0), (3, 0), (1, 1), (3, 1), (2, 0), (2, 1)]

    def owner_of(dx, dz):
        return place(4 - dx, dz)[0]

    def table_copy(source, half):
        at = sources.index(source) * HALVES + half
        return pltpu.make_async_remote_copy(
            src_ref=table.at[me, half], dst_ref=table.at[me, half],
            send_sem=table_send.at[at], recv_sem=table_recv.at[at],
            device_id=place(*source, half), device_id_type=MESH)

    def core_copy(source, half):
        at = (len(sources) if source is None else sources.index(source)) * HALVES + half + 14
        slot = me if source is None else owner_of(*source)
        return pltpu.make_async_remote_copy(
            src_ref=table.at[slot, half], dst_ref=table.at[slot, half],
            send_sem=table_send.at[at], recv_sem=table_recv.at[at],
            device_id=partner, device_id_type=MESH)

    def pick(slot):
        rows = table[slot].reshape(2 * ROWS, ROWS)
        base = slot * (2 * ROWS)
        hot = [jnp.where(offsets[...] == base + half * ROWS, 1.0, 0.0).astype(BF16) for half in range(HALVES)]
        return product(jnp.concatenate(hot, 1), rows)

    def other(slot):
        return slot + 1 - 2 * core

    for source in sources:
        for half in range(HALVES):
            table_copy(source, half).start()
    for half in range(HALVES):
        core_copy(None, half).start()
    for chunk in range(CHUNKS):
        load(chunk).start()
    picked[...] = pick(me)
    for half in range(HALVES):
        core_copy(None, half).wait_recv()
    picked[...] += pick(other(me))
    for source in sources:
        for half in range(HALVES):
            table_copy(source, half).wait_recv()
            core_copy(source, half).start()
        picked[...] += pick(owner_of(*source))
        at = sources.index(source)
        if at:
            for half in range(HALVES):
                core_copy(sources[at - 1], half).wait_recv()
            picked[...] += pick(other(owner_of(*sources[at - 1])))
    for half in range(HALVES):
        core_copy(sources[-1], half).wait_recv()
    picked[...] += pick(other(owner_of(*sources[-1])))

    parts = [picked[begin:begin + NORB] for begin in range(0, 4 * NORB, NORB)]
    real, imag = parts[:2]
    second_w[...] = jnp.concatenate(
        [jnp.concatenate([real, imag], 1), jnp.concatenate([-imag, real], 1)], 0).astype(BF16)
    real, imag = parts[2:]
    first_w[...] = jnp.concatenate(
        [jnp.concatenate([real, imag], 1).T, jnp.concatenate([imag, -real], 1).T], 1).astype(BF16)

    def sums_copy(block, part, offset):
        dy, dz = SUM_ORDER[offset - 1]
        peer = lax.rem(slab // 2 + dy, 4) * 2 + lax.rem(slab % 2 + dz, 2)
        return pltpu.make_async_remote_copy(
            src_ref=sums_out.at[block, part, peer], dst_ref=sums_in.at[block, part, slab],
            send_sem=sums_send.at[block, part, offset], recv_sem=sums_recv.at[block, part, offset],
            device_id=(me, peer), device_id_type=MESH)

    def clear():
        k_real[...] = jnp.zeros_like(k_real)
        k_cross[...] = jnp.zeros_like(k_cross)

    at = lax.broadcasted_iota(jnp.int32, (64, ROWS), 1)

    def send_sums(block, part):
        value = k_cross[...].T - k_cross[...] if part else k_real[...]
        value = (value * factor).reshape(8, 4, 8, NORB)
        for peer in range(NSLAB):
            tile, shift = peer // 4, peer % 4
            message = None
            for b in range(4):
                rows = value[:, b, :, tile * ROWS:(tile + 1) * ROWS].reshape(64, ROWS)
                turn = (b - shift) % 4 * 32
                if turn:
                    rows = pltpu.roll(rows, turn, 1)
                message = rows if message is None else jnp.where(at >= b * 32, rows, message)
            sums_out[block, part, peer] = message
        for offset in range(1, NSLAB):
            sums_copy(block, part, offset).start()

    clear()

    def left(group, carry):
        for chunk in range(GROUP // step):
            load(group * (GROUP // step) + chunk).wait()
        rounded = []
        for p in range(GROUP):
            both = jnp.concatenate([blocks[0, group * GROUP + p], blocks[1, group * GROUP + p]], 1)
            rounded.append(product(both, second_w[...]).astype(BF16))
        real = jnp.concatenate([x[:, :NOCC] for x in rounded], 1)
        imag = jnp.concatenate([x[:, NOCC:] for x in rounded], 1)
        terms = product_nt(jnp.concatenate([real, imag], 0), real)
        k_real[...] += terms[:NORB] + product_nt(imag, imag)
        k_cross[...] += terms[NORB:]
        return carry

    lax.fori_loop(0, naux // GROUP, left, 0)
    send_sums(0, 0)
    send_sums(0, 1)
    clear()

    def right(group, carry):
        rounded = []
        for p in range(GROUP):
            both = jnp.concatenate([blocks[0, group * GROUP + p], blocks[1, group * GROUP + p]], 0)
            rounded.append(product(first_w[...], both).astype(BF16))
        real = jnp.concatenate([x[:NOCC] for x in rounded], 0)
        imag = jnp.concatenate([x[NOCC:] for x in rounded], 0)
        turned = imag.T
        k_cross[...] += product(turned, real)
        kept[group, 0] = real
        kept[group, 1] = imag
        kept_turned[group, 0] = real.T
        kept_turned[group, 1] = turned
        return carry

    lax.fori_loop(0, naux // GROUP, right, 0, unroll=2)
    send_sums(1, 1)
    real = jnp.concatenate([kept[group, part] for group in range(naux // GROUP) for part in range(2)], 0)
    turned = jnp.concatenate([kept_turned[group, part] for group in range(naux // GROUP) for part in range(2)], 1)
    k_real[...] = product(turned, real)
    send_sums(1, 0)

    def total(block, part):
        sums_in[block, part, slab] = sums_out[block, part, slab]
        for offset in range(1, NSLAB):
            sums_copy(block, part, offset).wait_recv()
        value = sums_in[block, part, 0]
        for sender in range(1, NSLAB):
            value = value + sums_in[block, part, sender]
        return value

    def tile_copy(block, offset):
        dx, dz, dc = TILE_ORDER[offset - 1]
        peer = lax.rem(me // 4 + dx, 4) * 4 + lax.rem(me // 2 % 2 + dz, 2) * 2 + lax.rem(core + dc, 2)
        begin, rows = (0, 16) if block == 0 else (16, 8)
        return pltpu.make_async_remote_copy(
            src_ref=tiles_out.at[peer, pl.ds(begin, rows)], dst_ref=tiles_in.at[me, pl.ds(begin, rows)],
            send_sem=tiles_send.at[block, offset], recv_sem=tiles_recv.at[block, offset],
            device_id=(peer, slab), device_id_type=MESH)

    low = at < 64
    row = lax.broadcasted_iota(jnp.int32, (8, ROWS), 0)
    tiles_out[:, 8:16] = jnp.broadcast_to(jnp.where(row == 0, first_k, second_k).astype(F32), (NPAIR, 8, ROWS))
    for block in range(2):
        parts = [None, None]
        for part in ((0, 1) if block == 0 else (1, 0)):
            parts[part] = total(block, part)
        real, imag = parts
        even = jnp.where(low, real, pltpu.roll(imag, 64, 1)).reshape(8, 8, ROWS)
        odd = jnp.where(low, pltpu.roll(real, 64, 1), imag).reshape(8, 8, ROWS)
        begin = block * 16
        for pair in range(NPAIR):
            tiles_out[pair, begin:begin + 8] = (odd if pair % 2 else even)[pair // 2]
        for offset in range(1, NPAIR):
            tile_copy(block, offset).start()
    tiles_in[me] = tiles_out[me]
    bins = [jnp.zeros((8, ROWS), F32) for k in range(NKPT)]
    for block in range(2):
        for offset in range(1, NPAIR):
            tile_copy(block, offset).wait_recv()
        for owner in range(NPAIR):
            tile = tiles_in[owner, block * 16:block * 16 + 8]
            kpoint = tiles_in[owner, 8 + block:9 + block]
            bins = [bins[k] + jnp.where(kpoint == k, tile, 0.0) for k in range(NKPT)]
    for k in range(NKPT):
        for part in range(2):
            for upper in range(2):
                begin = part * 64 + upper * 32
                out_ref[part, k, upper * 8:upper * 8 + 8] = bins[k][:, begin:begin + 32]

    for half in range(HALVES):
        core_copy(None, half).wait_send()
        for source in sources:
            table_copy(source, half).wait_send()
            core_copy(source, half).wait_send()
    for block in range(2):
        for offset in range(1, NPAIR):
            tile_copy(block, offset).wait_send()
        for part in range(2):
            for offset in range(1, NSLAB):
                sums_copy(block, part, offset).wait_send()


def local(integrals, coef_table, row_slot, pair_k):
    naux = integrals.shape[2]
    blocks = integrals.reshape(integrals.shape[1:])
    out = pl.pallas_call(
        kernel,
        out_shape=jax.ShapeDtypeStruct((2, NKPT, 16, 32), F32),
        in_specs=[pl.BlockSpec(memory_space=pl.ANY)] * 4,
        out_specs=pl.BlockSpec(memory_space=pltpu.VMEM),
        scratch_shapes=[
            pltpu.SMEM((1, 2), jnp.int32),
            pltpu.VMEM((16, ROWS), jnp.int32),
            pltpu.VMEM((2, naux, NORB, NORB), BF16),
            pltpu.VMEM((NPAIR, HALVES, ROWS, ROWS), BF16),
            pltpu.VMEM((4 * NORB, ROWS), jnp.int32),
            pltpu.VMEM((4 * NORB, ROWS), F32),
            pltpu.VMEM((2 * NORB, NORB), BF16),
            pltpu.VMEM((NORB, 2 * NORB), BF16),
            pltpu.VMEM((naux // GROUP, 2, GROUP * NOCC, NORB), BF16),
            pltpu.VMEM((naux // GROUP, 2, NORB, GROUP * NOCC), BF16),
            pltpu.VMEM((NORB, NORB), F32),
            pltpu.VMEM((NORB, NORB), F32),
            pltpu.VMEM((2, 2, NSLAB, 64, ROWS), F32),
            pltpu.VMEM((2, 2, NSLAB, 64, ROWS), F32),
            pltpu.VMEM((NPAIR, 24, ROWS), F32),
            pltpu.VMEM((NPAIR, 24, ROWS), F32),
            pltpu.SemaphoreType.DMA((CHUNKS + 3,)),
            pltpu.SemaphoreType.DMA((30,)),
            pltpu.SemaphoreType.DMA((30,)),
            pltpu.SemaphoreType.DMA((2, 2, NSLAB)),
            pltpu.SemaphoreType.DMA((2, 2, NSLAB)),
            pltpu.SemaphoreType.DMA((2, NPAIR)),
            pltpu.SemaphoreType.DMA((2, NPAIR)),
        ],
        compiler_params=pltpu.CompilerParams(
            collective_id=0, has_side_effects=True, vmem_limit_bytes=56 * 2**20),
    )(pair_k, coef_table.reshape(HALVES, ROWS, ROWS), row_slot.reshape(16, ROWS), blocks)
    return out.transpose(0, 1, 3, 2)


def solution(mesh):
    in_specs = (P("pair", None, "aux", None, None), P("pair", None, None), P(), P("pair", None))
    out_specs = P(None, None, "aux", "pair")
    return jax.shard_map(local, mesh=mesh, in_specs=in_specs, out_specs=out_specs, check_vma=False)
```

```python
import jax
import jax.numpy as jnp
from jax import lax
from jax.experimental import pallas as pl
from jax.experimental.pallas import tpu as pltpu
from jax.sharding import PartitionSpec as P

NKPT = 8
NORB = 256
NOCC = 128
NPAIR = 16
NSLAB = 8
ROWS = 128
HALVES = 2
GROUP = 16
CHUNKS = 8
F32 = jnp.float32
BF16 = jnp.bfloat16
MESH = pl.DeviceIdType.MESH
SUM_ORDER = ((2, 1), (1, 1), (3, 1), (2, 0), (0, 1), (1, 0), (3, 0))
TILE_ORDER = tuple((dx, dz, dc) for dx, dz in ((2, 1), (2, 0), (1, 1), (3, 1), (0, 1), (1, 0), (3, 0)) for dc in (0, 1)) + ((0, 0, 1),)


def product(left, right):
    return lax.dot_general(left, right, (((1,), (0,)), ((), ())), preferred_element_type=F32)


def product_nt(left, right):
    return lax.dot_general(left, right, (((1,), (1,)), ((), ())), preferred_element_type=F32)


def product_tn(left, right):
    return lax.dot_general(left, right, (((0,), (0,)), ((), ())), preferred_element_type=F32)


def places(me, slab):
    x, low, core = me // 4, me // 2 % 2, me % 2
    y, high = slab // 2, slab % 2
    beyond = (y * 2 + lax.rem(high + low, 2), y * 2 + lax.rem(high + 1 - low, 2))

    def place(dx, dz=0, way=0):
        pair = lax.rem(x + dx, 4) * 4 + (1 - low if dz else low) * 2 + core
        return pair, (beyond[way] if dz else slab)

    return place


def kernel(pair_hbm, piece_hbm, slot_hbm, blocks_ref, out_ref, pair_ref, slot_ref, blocks, table, offsets, picked,
           second_w, first_w, kept, kept_turned, k_real, k_cross, sums_out, sums_in, tiles_out, tiles_in,
           load_sem, table_send, table_recv, sums_send, sums_recv, tiles_send, tiles_recv):
    me = lax.axis_index("pair")
    slab = lax.axis_index("aux")
    naux = blocks.shape[1]
    step = naux // CHUNKS
    factor = 1.0 / (naux * NSLAB * NOCC)
    place = places(me, slab)
    core = me % 2
    partner = (me + 1 - 2 * core, slab)

    def load(chunk):
        span = pl.ds(chunk * step, step)
        return pltpu.make_async_copy(blocks_ref.at[:, span], blocks.at[:, span], load_sem.at[chunk])

    barrier = pltpu.get_barrier_semaphore()
    beyond = (slab // 2) * 2 + 1 - slab % 2
    greeted = [(place(dx, 1)[0], beyond) for dx in range(4)]
    greeted += [(lax.rem(me + offset, NPAIR), slab) for offset in range(1, NPAIR)]
    greeted += [(me, lax.rem(slab + offset, NSLAB)) for offset in range(1, NSLAB)]
    for peer in greeted:
        pl.semaphore_signal(barrier, inc=1, device_id=peer, device_id_type=MESH)

    small = [pltpu.make_async_copy(pair_hbm, pair_ref, load_sem.at[CHUNKS]),
             pltpu.make_async_copy(slot_hbm, slot_ref, load_sem.at[CHUNKS + 1]),
             pltpu.make_async_copy(piece_hbm, table.at[me], load_sem.at[CHUNKS + 2])]
    for copy in small:
        copy.start()
    for copy in small:
        copy.wait()
    for chunk in range(CHUNKS):
        load(chunk).start()

    first_k = pair_ref[0, 0]
    second_k = pair_ref[0, 1]
    slots = slot_ref[...]
    lane = lax.broadcasted_iota(jnp.int32, (ROWS, ROWS), 1)
    for at, kpoint in enumerate((second_k, first_k)):
        for half in range(2):
            row = jnp.zeros((1, ROWS), jnp.int32)
            for k in range(NKPT):
                row = jnp.where(kpoint == k, slots[2 * k + half:2 * k + half + 1], row)
            where = 2 * jnp.broadcast_to(row, (ROWS, ROWS)).T - lane
            for part in range(2):
                begin = (at * 4 + part * 2 + half) * ROWS
                offsets[begin:begin + ROWS] = where + part

    pl.semaphore_wait(barrier, len(greeted))

    sources = [(0, 1), (1, 0), (3, 0), (1, 1), (3, 1), (2, 0), (2, 1)]

    def owner_of(dx, dz):
        return place(4 - dx, dz)[0]

    def table_copy(source, half):
        at = sources.index(source) * HALVES + half
        return pltpu.make_async_remote_copy(
            src_ref=table.at[me, half], dst_ref=table.at[me, half],
            send_sem=table_send.at[at], recv_sem=table_recv.at[at],
            device_id=place(*source, half), device_id_type=MESH)

    def core_copy(source, half):
        at = (len(sources) if source is None else sources.index(source)) * HALVES + half + 14
        slot = me if source is None else owner_of(*source)
        return pltpu.make_async_remote_copy(
            src_ref=table.at[slot, half], dst_ref=table.at[slot, half],
            send_sem=table_send.at[at], recv_sem=table_recv.at[at],
            device_id=partner, device_id_type=MESH)

    def pick(slot):
        rows = table[slot].reshape(2 * ROWS, ROWS)
        base = slot * (2 * ROWS)
        hot = [jnp.where(offsets[...] == base + half * ROWS, 1.0, 0.0).astype(BF16) for half in range(HALVES)]
        return product(jnp.concatenate(hot, 1), rows)

    def other(slot):
        return slot + 1 - 2 * core

    for source in sources:
        for half in range(HALVES):
            table_copy(source, half).start()
    for half in range(HALVES):
        core_copy(None, half).start()
    picked[...] = pick(me)
    for half in range(HALVES):
        core_copy(None, half).wait_recv()
    picked[...] += pick(other(me))
    for source in sources:
        for half in range(HALVES):
            table_copy(source, half).wait_recv()
            core_copy(source, half).start()
        picked[...] += pick(owner_of(*source))
        at = sources.index(source)
        if at:
            for half in range(HALVES):
                core_copy(sources[at - 1], half).wait_recv()
            picked[...] += pick(other(owner_of(*sources[at - 1])))
    for half in range(HALVES):
        core_copy(sources[-1], half).wait_recv()
    picked[...] += pick(other(owner_of(*sources[-1])))

    parts = [picked[begin:begin + NORB] for begin in range(0, 4 * NORB, NORB)]
    real, imag = parts[:2]
    second_w[...] = jnp.concatenate(
        [jnp.concatenate([real, imag], 1), jnp.concatenate([-imag, real], 1)], 0).astype(BF16)
    real, imag = parts[2:]
    first_w[...] = jnp.concatenate(
        [jnp.concatenate([real, imag], 1).T, jnp.concatenate([imag, -real], 1).T], 1).astype(BF16)

    def sums_copy(block, part, offset):
        dy, dz = SUM_ORDER[offset - 1]
        peer = lax.rem(slab // 2 + dy, 4) * 2 + lax.rem(slab % 2 + dz, 2)
        return pltpu.make_async_remote_copy(
            src_ref=sums_out.at[block, part, peer], dst_ref=sums_in.at[block, part, slab],
            send_sem=sums_send.at[block, part, offset], recv_sem=sums_recv.at[block, part, offset],
            device_id=(me, peer), device_id_type=MESH)

    def clear():
        k_real[...] = jnp.zeros_like(k_real)
        k_cross[...] = jnp.zeros_like(k_cross)

    at = lax.broadcasted_iota(jnp.int32, (64, ROWS), 1)

    def send_sums(block, part):
        value = k_cross[...].T - k_cross[...] if part else k_real[...]
        value = (value * factor).reshape(8, 4, 8, NORB)
        for peer in range(NSLAB):
            tile, shift = peer // 4, peer % 4
            message = None
            for b in range(4):
                rows = value[:, b, :, tile * ROWS:(tile + 1) * ROWS].reshape(64, ROWS)
                turn = (b - shift) % 4 * 32
                if turn:
                    rows = pltpu.roll(rows, turn, 1)
                message = rows if message is None else jnp.where(at >= b * 32, rows, message)
            sums_out[block, part, peer] = message
        for offset in range(1, NSLAB):
            sums_copy(block, part, offset).start()

    clear()

    def left(group, carry):
        for chunk in range(GROUP // step):
            load(group * (GROUP // step) + chunk).wait()
        rounded = []
        for p in range(GROUP):
            both = jnp.concatenate([blocks[0, group * GROUP + p], blocks[1, group * GROUP + p]], 1)
            rounded.append(product(both, second_w[...]).astype(BF16))
        real = jnp.concatenate([x[:, :NOCC] for x in rounded], 1)
        imag = jnp.concatenate([x[:, NOCC:] for x in rounded], 1)
        terms = product_nt(jnp.concatenate([real, imag], 0), real)
        k_real[...] += terms[:NORB] + product_nt(imag, imag)
        k_cross[...] += terms[NORB:]
        return carry

    lax.fori_loop(0, naux // GROUP, left, 0)
    send_sums(0, 0)
    send_sums(0, 1)
    clear()

    def right(group, carry):
        rounded = []
        for p in range(GROUP):
            both = jnp.concatenate([blocks[0, group * GROUP + p], blocks[1, group * GROUP + p]], 0)
            rounded.append(product(first_w[...], both).astype(BF16))
        real = jnp.concatenate([x[:NOCC] for x in rounded], 0)
        imag = jnp.concatenate([x[NOCC:] for x in rounded], 0)
        turned = imag.T
        k_cross[...] += product(turned, real)
        kept[group, 0] = real
        kept[group, 1] = imag
        kept_turned[group, 0] = real.T
        kept_turned[group, 1] = turned
        return carry

    lax.fori_loop(0, naux // GROUP, right, 0, unroll=2)
    send_sums(1, 1)
    real = jnp.concatenate([kept[group, part] for group in range(naux // GROUP) for part in range(2)], 0)
    turned = jnp.concatenate([kept_turned[group, part] for group in range(naux // GROUP) for part in range(2)], 1)
    k_real[...] = product(turned, real)
    send_sums(1, 0)

    def total(block, part):
        sums_in[block, part, slab] = sums_out[block, part, slab]
        for offset in range(1, NSLAB):
            sums_copy(block, part, offset).wait_recv()
        value = sums_in[block, part, 0]
        for sender in range(1, NSLAB):
            value = value + sums_in[block, part, sender]
        return value

    def tile_copy(block, offset):
        dx, dz, dc = TILE_ORDER[offset - 1]
        peer = lax.rem(me // 4 + dx, 4) * 4 + lax.rem(me // 2 % 2 + dz, 2) * 2 + lax.rem(core + dc, 2)
        begin, rows = (0, 16) if block == 0 else (16, 8)
        return pltpu.make_async_remote_copy(
            src_ref=tiles_out.at[peer, pl.ds(begin, rows)], dst_ref=tiles_in.at[me, pl.ds(begin, rows)],
            send_sem=tiles_send.at[block, offset], recv_sem=tiles_recv.at[block, offset],
            device_id=(peer, slab), device_id_type=MESH)

    low = at < 64
    row = lax.broadcasted_iota(jnp.int32, (8, ROWS), 0)
    tiles_out[:, 8:16] = jnp.broadcast_to(jnp.where(row == 0, first_k, second_k).astype(F32), (NPAIR, 8, ROWS))
    for block in range(2):
        parts = [None, None]
        for part in ((0, 1) if block == 0 else (1, 0)):
            parts[part] = total(block, part)
        real, imag = parts
        even = jnp.where(low, real, pltpu.roll(imag, 64, 1)).reshape(8, 8, ROWS)
        odd = jnp.where(low, pltpu.roll(real, 64, 1), imag).reshape(8, 8, ROWS)
        begin = block * 16
        for pair in range(NPAIR):
            tiles_out[pair, begin:begin + 8] = (odd if pair % 2 else even)[pair // 2]
        for offset in range(1, NPAIR):
            tile_copy(block, offset).start()
    tiles_in[me] = tiles_out[me]
    bins = [jnp.zeros((8, ROWS), F32) for k in range(NKPT)]
    for block in range(2):
        for offset in range(1, NPAIR):
            tile_copy(block, offset).wait_recv()
        for owner in range(NPAIR):
            tile = tiles_in[owner, block * 16:block * 16 + 8]
            kpoint = tiles_in[owner, 8 + block:9 + block]
            bins = [bins[k] + jnp.where(kpoint == k, tile, 0.0) for k in range(NKPT)]
    for k in range(NKPT):
        for part in range(2):
            for upper in range(2):
                begin = part * 64 + upper * 32
                out_ref[part, k, upper * 8:upper * 8 + 8] = bins[k][:, begin:begin + 32]

    for half in range(HALVES):
        core_copy(None, half).wait_send()
        for source in sources:
            table_copy(source, half).wait_send()
            core_copy(source, half).wait_send()
    for block in range(2):
        for offset in range(1, NPAIR):
            tile_copy(block, offset).wait_send()
        for part in range(2):
            for offset in range(1, NSLAB):
                sums_copy(block, part, offset).wait_send()


def local(integrals, coef_table, row_slot, pair_k):
    naux = integrals.shape[2]
    blocks = integrals.reshape(integrals.shape[1:])
    out = pl.pallas_call(
        kernel,
        out_shape=jax.ShapeDtypeStruct((2, NKPT, 16, 32), F32),
        in_specs=[pl.BlockSpec(memory_space=pl.ANY)] * 4,
        out_specs=pl.BlockSpec(memory_space=pltpu.VMEM),
        scratch_shapes=[
            pltpu.SMEM((1, 2), jnp.int32),
            pltpu.VMEM((16, ROWS), jnp.int32),
            pltpu.VMEM((2, naux, NORB, NORB), BF16),
            pltpu.VMEM((NPAIR, HALVES, ROWS, ROWS), BF16),
            pltpu.VMEM((4 * NORB, ROWS), jnp.int32),
            pltpu.VMEM((4 * NORB, ROWS), F32),
            pltpu.VMEM((2 * NORB, NORB), BF16),
            pltpu.VMEM((NORB, 2 * NORB), BF16),
            pltpu.VMEM((naux // GROUP, 2, GROUP * NOCC, NORB), BF16),
            pltpu.VMEM((naux // GROUP, 2, NORB, GROUP * NOCC), BF16),
            pltpu.VMEM((NORB, NORB), F32),
            pltpu.VMEM((NORB, NORB), F32),
            pltpu.VMEM((2, 2, NSLAB, 64, ROWS), F32),
            pltpu.VMEM((2, 2, NSLAB, 64, ROWS), F32),
            pltpu.VMEM((NPAIR, 24, ROWS), F32),
            pltpu.VMEM((NPAIR, 24, ROWS), F32),
            pltpu.SemaphoreType.DMA((CHUNKS + 3,)),
            pltpu.SemaphoreType.DMA((30,)),
            pltpu.SemaphoreType.DMA((30,)),
            pltpu.SemaphoreType.DMA((2, 2, NSLAB)),
            pltpu.SemaphoreType.DMA((2, 2, NSLAB)),
            pltpu.SemaphoreType.DMA((2, NPAIR)),
            pltpu.SemaphoreType.DMA((2, NPAIR)),
        ],
        compiler_params=pltpu.CompilerParams(
            collective_id=0, has_side_effects=True, vmem_limit_bytes=56 * 2**20),
    )(pair_k, coef_table.reshape(HALVES, ROWS, ROWS), row_slot.reshape(16, ROWS), blocks)
    return out.transpose(0, 1, 3, 2)


def solution(mesh):
    in_specs = (P("pair", None, "aux", None, None), P("pair", None, None), P(), P("pair", None))
    out_specs = P(None, None, "aux", "pair")
    return jax.shard_map(local, mesh=mesh, in_specs=in_specs, out_specs=out_specs, check_vma=False)
```
